512 devices in a mesh: row: 16 (over z, y_hi), col: 32 (over x, y_lo, core).
Axes of the slice: x: 4, y: 8 (y_hi: 2, y_lo: 4; y = y_hi * 4 + y_lo), z: 8, core: 2. Of those that a mesh axis runs over, the one named last changes fastest.
Arguments:
- scalars: float32 [1, 256, 256, 512], P(None, 'row', 'col'), may hold values from -6 to 6
- velocity: bfloat16 [3, 256, 256, 512], P(None, 'row', 'col'), may hold values from -6 to 6
- first_x: bfloat16 [512, 512], replicated, may hold values from -0.25 to 0.25
- second_x: bfloat16 [512, 512], replicated, may hold values from -0.25 to 0.25
- first_y: bfloat16 [256, 256], replicated, may hold values from -0.375 to 0.375
- second_y: bfloat16 [256, 256], replicated, may hold values from -0.375 to 0.375
- first_z: bfloat16 [256, 256], replicated, may hold values from -0.375 to 0.375
- second_z: bfloat16 [256, 256], replicated, may hold values from -0.375 to 0.375
Outputs:
- updated: float32 [1, 256, 256, 512], P(None, 'row', 'col')
The draws below stay inside these ranges and needn't reach their ends.
All inputs are finite; a program needn't handle non-finite values.
Results may differ from the reference program's by a relative error of at most 0.0021.
Values may be sent and summed in bfloat16 or wider, within the bound.
No kernel may reach another device: no remote copies, remote signals or barrier semaphores. Data moves between devices by JAX's collectives and lax.ppermute only.
A program may use at most 64 MiB of HBM per device.

```python
import jax
import jax.numpy as jnp
from jax import lax

NX = 512
NY = 256
NZ = 256
NS = 1


def levels(key, extent, pieces, smallest, largest):
    gain, own = 1.0, jax.random.fold_in(key, 6)
    for axis_at, shards_of in pieces:
        draws = jnp.exp(jax.random.uniform(jax.random.fold_in(own, axis_at), (shards_of,), jnp.float32, smallest / len(pieces), largest / len(pieces)))
        gain = gain * jnp.repeat(draws, extent[axis_at] // shards_of).reshape([-1 if axis == axis_at else 1 for axis in range(len(extent))])
    return gain


def centred(stream_key, extent, spread, reach, shards=(), dtype=jnp.bfloat16):
    entries = jax.random.normal(stream_key, extent, jnp.float32) * spread
    if len(shards) > 0:
        entries = levels(stream_key, extent, shards, -0.22, 0.18) * entries
    return jnp.clip(entries, min=-reach, max=reach).astype(dtype)


def setup_inputs(seed: int = 0) -> dict:
    keys = jax.random.split(jax.random.key(seed), 9)
    scalars = centred(keys[0], (NS, NY, NZ, NX), 1.0, 6.0, ((1, 16), (2, 32)), jnp.float32)
    velocity = centred(keys[1], (3, NY, NZ, NX), 1.0, 6.0, ((1, 16), (2, 32)))
    first_x = centred(keys[2], (NX, NX), NX ** -0.5, 0.25)
    second_x = centred(keys[3], (NX, NX), NX ** -0.5, 0.25)
    first_y = centred(keys[4], (NY, NY), NY ** -0.5, 0.375)
    second_y = centred(keys[5], (NY, NY), NY ** -0.5, 0.375)
    first_z = centred(keys[6], (NZ, NZ), NZ ** -0.5, 0.375)
    second_z = centred(keys[7], (NZ, NZ), NZ ** -0.5, 0.375)
    return {"scalars": scalars, "velocity": velocity, "first_x": first_x, "second_x": second_x, "first_y": first_y, "second_y": second_y, "first_z": first_z, "second_z": second_z}


diffusion_coefficient = 0.5
step_weight = 0.5


def apply_along(scalar_values, matrix, spatial_axis):
    shifted = jnp.moveaxis(scalar_values, spatial_axis, -1)
    result = jnp.dot(shifted, matrix.T, preferred_element_type=jnp.float32)
    return jnp.moveaxis(result, -1, spatial_axis)


def one_scalar(scalar_values, velocity, first_x, second_x, first_y, second_y, first_z, second_z):
    compiled_step = scalar_values.astype(jnp.bfloat16)
    tendency_sum = jnp.zeros_like(scalar_values)
    solver_options = ((velocity[0], first_x, second_x, 2), (velocity[1], first_y, second_y, 0), (velocity[2], first_z, second_z, 1))
    for velocity_field, first_derivative_matrix, second_derivative_matrix, spatial_axis in solver_options:
        velocity_flux = velocity_field.astype(jnp.float32)
        flux_product = (velocity_flux * compiled_step.astype(jnp.float32)).astype(jnp.bfloat16)
        scalar_gradient = apply_along(compiled_step, first_derivative_matrix, spatial_axis)
        advected_scalar = apply_along(flux_product, first_derivative_matrix, spatial_axis)
        second_derivative = apply_along(compiled_step, second_derivative_matrix, spatial_axis)
        tendency_sum = tendency_sum + (-0.5 * (velocity_flux * scalar_gradient + advected_scalar) + diffusion_coefficient * second_derivative)
    return scalar_values + step_weight * tendency_sum


def reference(scalars, velocity, first_x, second_x, first_y, second_y, first_z, second_z):
    return lax.map(lambda scalar_values: one_scalar(scalar_values, velocity, first_x, second_x, first_y, second_y, first_z, second_z), scalars)
```

```python
import jax
import jax.numpy as jnp
from jax import lax
from jax.experimental import pallas as pl
from jax.experimental.pallas import tpu as pltpu
from jax.sharding import PartitionSpec as P

LANES = 128
VMEM = pl.BlockSpec(memory_space=pltpu.VMEM)


def call(kernel, out_shape, scratch_shapes=()):
    shapes = out_shape if isinstance(out_shape, list) else [out_shape]
    run = pl.pallas_call(
        kernel,
        out_shape=out_shape,
        out_specs=[VMEM] * len(shapes) if isinstance(out_shape, list) else VMEM,
        scratch_shapes=list(scratch_shapes),
        name=kernel.__name__,
    )
    return run


def pack_kernel(s_ref, v_ref, w_ref, row_ref, col_ref, s32, v32):
    ny, nz, nx = s_ref.shape
    half = nx // 2
    for t in range(nx // LANES):
        h, at = divmod(t * LANES, half)
        lanes = slice(t * LANES, (t + 1) * LANES)
        to = slice(at, at + LANES)
        s = s_ref[:, :, lanes]
        s32[t] = s.reshape(ny * nz, LANES)
        v32[t] = v_ref[:, :, lanes].astype(jnp.float32).reshape(ny * nz, LANES)
        col_ref[:, h, 0, :, to] = s.astype(jnp.bfloat16)
        col_ref[:, h, 1, :, to] = w_ref[:, :, lanes]
        for z in range(nz):
            row_ref[2 * z + h, 0, :, to] = s32[t, pl.ds(z, ny, stride=nz), :].astype(jnp.bfloat16)
            row_ref[2 * z + h, 1, :, to] = v32[t, pl.ds(z, ny, stride=nz), :].astype(jnp.bfloat16)


def dot(a, b):
    return lax.dot_general(a, b, (((1,), (0,)), ((), ())), preferred_element_type=jnp.float32)


def line_kernel(r_ref, first_ref, second_ref, out_ref):
    blocks, _, depth, lanes = r_ref.shape
    s = r_ref[:, 0].reshape(blocks * depth, lanes)
    c = r_ref[:, 1].reshape(blocks * depth, lanes).astype(jnp.float32)
    flux = (c * s.astype(jnp.float32)).astype(jnp.bfloat16)
    first = first_ref[...]
    term = -0.5 * (c * dot(first, s) + dot(first, flux)) + 0.5 * dot(second_ref[...], s)
    out_ref[...] = term.astype(jnp.bfloat16).reshape(blocks, depth, lanes)


def dot_t(a, b):
    return lax.dot_general(a, b, (((1,), (1,)), ((), ())), preferred_element_type=jnp.float32)


def x_kernel(s_ref, u_ref, first_ref, second_ref, out_ref):
    ny, nz, nx = s_ref.shape
    s = s_ref[...].reshape(ny * nz, nx)
    sb = s.astype(jnp.bfloat16)
    u = u_ref[...].astype(jnp.float32).reshape(ny * nz, nx)
    flux = (u * sb.astype(jnp.float32)).astype(jnp.bfloat16)
    first = first_ref[...]
    term = -0.5 * (u * dot_t(sb, first) + dot_t(flux, first)) + 0.5 * dot_t(sb, second_ref[...])
    out_ref[...] = (s + 0.5 * term).reshape(ny, nz, nx)


def final_kernel(base_ref, y_ref, z_ref, out_ref, y32):
    ny, nz, nx = base_ref.shape
    half = nx // 2
    for t in range(nx // LANES):
        h, at = divmod(t * LANES, half)
        lanes = slice(t * LANES, (t + 1) * LANES)
        of = slice(at, at + LANES)
        for z in range(nz):
            y32[t, pl.ds(z, ny, stride=nz), :] = y_ref[2 * z + h, :, of].astype(jnp.float32)
        y = y32[t].reshape(ny, nz, LANES)
        out_ref[:, :, lanes] = base_ref[:, :, lanes] + 0.5 * (y + z_ref[:, h, :, of].astype(jnp.float32))


def body(scalars, velocity, first_x, second_x, first_y, second_y, first_z, second_z):
    _, ny, nz, nx = scalars.shape
    rows, cols = lax.axis_size("row"), lax.axis_size("col")
    half = nx // 2
    s = scalars[0]
    u, v, w = velocity[0], velocity[1], velocity[2]
    bf16, f32 = jnp.bfloat16, jnp.float32
    row_send, col_send = call(
        pack_kernel,
        [jax.ShapeDtypeStruct((rows, 2, ny, half), bf16), jax.ShapeDtypeStruct((ny, 2, 2, nz, half), bf16)],
        [pltpu.VMEM((nx // LANES, ny * nz, LANES), f32)] * 2,
    )(s, v, w)
    col_send = col_send.reshape(cols, 2, nz, half)
    row_in = lax.all_to_all(row_send, "row", split_axis=0, concat_axis=0, tiled=True)
    col_in = lax.all_to_all(col_send, "col", split_axis=0, concat_axis=0, tiled=True)
    base = call(x_kernel, jax.ShapeDtypeStruct((ny, nz, nx), f32))(s, u, first_x, second_x)
    y_term = call(line_kernel, jax.ShapeDtypeStruct((rows, ny, half), bf16))(row_in, first_y, second_y)
    z_term = call(line_kernel, jax.ShapeDtypeStruct((cols, nz, half), bf16))(col_in, first_z, second_z)
    y_back = lax.all_to_all(y_term, "row", split_axis=0, concat_axis=0, tiled=True)
    z_back = lax.all_to_all(z_term, "col", split_axis=0, concat_axis=0, tiled=True)
    out = call(
        final_kernel,
        jax.ShapeDtypeStruct((ny, nz, nx), f32),
        [pltpu.VMEM((nx // LANES, ny * nz, LANES), f32)],
    )(base, y_back, z_back.reshape(ny, 2, nz, half))
    return out[None]


def solution(mesh):
    return jax.shard_map(
        body,
        mesh=mesh,
        in_specs=(
            P(None, "row", "col", None),
            P(None, "row", "col", None),
            P(),
            P(),
            P(),
            P(),
            P(),
            P(),
        ),
        out_specs=P(None, "row", "col", None),
        check_vma=False,
    )
```

```python
import jax
import jax.numpy as jnp
from jax import lax
from jax.experimental import pallas as pl
from jax.experimental.pallas import tpu as pltpu
from jax.sharding import Mesh
from jax.sharding import PartitionSpec as P


LANES = 128
VMEM = pl.BlockSpec(memory_space=pltpu.VMEM)
SMEM = pl.BlockSpec(memory_space=pltpu.SMEM)
BF16, F32 = jnp.bfloat16, jnp.float32


def component(shape, index):
    return pl.BlockSpec((None,) + shape[1:], lambda i: (index,) + (0,) * (len(shape) - 1))


def near(array):
    return pltpu.with_memory_space_constraint(array, pltpu.VMEM)


def dot(a, b, side):
    return lax.dot_general(a, b, (((1,), (side,)), ((), ())), preferred_element_type=F32)


def term_of(s, c, first, second, product):
    flux = (c * s.astype(F32)).astype(BF16)
    return -0.5 * (c * product(first, s) + product(first, flux)) + 0.5 * product(second, s)


def pack_kernel(high_ref, s_ref, v_ref, w_ref, keep_ref, give_ref, col_ref, s32, v32):
    ny, nz, nx = s_ref.shape
    half = nx // 2
    high = high_ref[0]
    for t in range(half // LANES):
        at = slice(t * LANES, (t + 1) * LANES)
        for h in range(2):
            lanes = slice(h * half + t * LANES, h * half + (t + 1) * LANES)
            s = s_ref[:, :, lanes]
            s32[h] = s.reshape(ny * nz, LANES)
            v32[h] = v_ref[:, :, lanes].astype(F32).reshape(ny * nz, LANES)
            col_ref[:, h, 0, :, at] = s.astype(BF16)
            col_ref[:, h, 1, :, at] = w_ref[:, :, lanes]
        for z in range(nz):
            for f, source in enumerate((s32, v32)):
                keep_ref[z, f, :, at] = source[high, pl.ds(z, ny, stride=nz), :].astype(BF16)
                give_ref[z, f, :, at] = source[1 - high, pl.ds(z, ny, stride=nz), :].astype(BF16)


def join_kernel(own_ref, other_ref, out_ref):
    out_ref[:, 0] = own_ref[...]
    out_ref[:, 1] = other_ref[...]


def x_kernel(s_ref, u_ref, first_ref, second_ref, out_ref):
    ny, nz, nx = s_ref.shape
    s = s_ref[...].reshape(ny * nz, nx)
    u = u_ref[...].astype(F32).reshape(ny * nz, nx)
    term = term_of(s.astype(BF16), u, first_ref[...], second_ref[...], lambda m, f: dot(f, m, 1))
    out_ref[...] = (s + 0.5 * term).reshape(ny, nz, nx)


def y_kernel(high_ref, r_ref, first_ref, second_ref, out_ref):
    blocks, _, _, depth, lanes = r_ref.shape
    high = high_ref[0]
    field = []
    for f in range(2):
        parts = [r_ref[:, high, f], r_ref[:, 1 - high, f]]
        field.append(jnp.stack(parts, axis=1).reshape(blocks * 2 * depth, lanes))
    s, c = field
    term = term_of(s, c.astype(F32), first_ref[...], second_ref[...], lambda m, f: dot(m, f, 0))
    term = term.astype(BF16).reshape(blocks, 2, depth, lanes)
    for slot in range(2):
        out_ref[:, high if slot == 0 else 1 - high] = term[:, slot]


def z_kernel(r_ref, first_ref, second_ref, out_ref):
    blocks, _, depth, lanes = r_ref.shape
    s = r_ref[:, 0].reshape(blocks * depth, lanes)
    c = r_ref[:, 1].reshape(blocks * depth, lanes).astype(F32)
    term = term_of(s, c, first_ref[...], second_ref[...], lambda m, f: dot(m, f, 0))
    out_ref[...] = term.astype(BF16).reshape(blocks, depth, lanes)


def final_kernel(high_ref, base_ref, own_ref, other_ref, z_ref, out_ref, y32):
    ny, nz, nx = base_ref.shape
    half = nx // 2
    high = high_ref[0]
    for t in range(half // LANES):
        at = slice(t * LANES, (t + 1) * LANES)
        for z in range(nz):
            y32[high, pl.ds(z, ny, stride=nz), :] = own_ref[z, 0, :, at].astype(F32)
            y32[1 - high, pl.ds(z, ny, stride=nz), :] = other_ref[z, :, at].astype(F32)
        for h in range(2):
            lanes = slice(h * half + t * LANES, h * half + (t + 1) * LANES)
            y = y32[h].reshape(ny, nz, LANES)
            out_ref[:, :, lanes] = base_ref[:, :, lanes] + 0.5 * (y + z_ref[:, h, :, at].astype(F32))


def body(scalars, velocity, first_x, second_x, first_y, second_y, first_z, second_z):
    _, ny, nz, nx = scalars.shape
    half = nx // 2
    blocks = lax.axis_size("z")
    cols = lax.axis_size("x") * lax.axis_size("l") * lax.axis_size("c")
    high = lax.axis_index("h").reshape(1)
    s = scalars[0]
    whole = pl.BlockSpec((ny, nz, nx), lambda i: (0, 0, 0))

    def partner(array):
        return lax.ppermute(array, "h", [(0, 1), (1, 0)])

    def exchange(array, axes):
        return lax.all_to_all(array, axes, split_axis=0, concat_axis=0, tiled=True)

    keep, give, col_send = pl.pallas_call(
        pack_kernel,
        grid=(1,),
        in_specs=[SMEM, whole, component(velocity.shape, 1), component(velocity.shape, 2)],
        out_specs=[VMEM] * 3,
        out_shape=[
            pltpu.VMEM((blocks, 2, ny, half), BF16),
            pltpu.VMEM((blocks, 2, ny, half), BF16),
            pltpu.VMEM((ny, 2, 2, nz, half), BF16),
        ],
        scratch_shapes=[pltpu.VMEM((2, ny * nz, LANES), F32)] * 2,
        name="pack",
    )(high, s, velocity, velocity)
    other = partner(give)
    col_in = exchange(col_send.reshape(cols, 2, nz, half), ("x", "l", "c"))
    row_send = pl.pallas_call(
        join_kernel,
        in_specs=[VMEM] * 2,
        out_specs=VMEM,
        out_shape=pltpu.VMEM((blocks, 2, 2, ny, half), BF16),
        name="join",
    )(near(keep), near(other))
    row_in = exchange(row_send, "z")
    base = pl.pallas_call(
        x_kernel,
        grid=(1,),
        in_specs=[whole, component(velocity.shape, 0), VMEM, VMEM],
        out_specs=VMEM,
        out_shape=pltpu.VMEM((ny, nz, nx), F32),
        name="xmath",
    )(s, velocity, near(first_x), near(second_x))
    z_term = pl.pallas_call(
        z_kernel,
        in_specs=[VMEM] * 3,
        out_specs=VMEM,
        out_shape=pltpu.VMEM((cols, nz, half), BF16),
        name="zmath",
    )(near(col_in), near(first_z), near(second_z))
    y_term = pl.pallas_call(
        y_kernel,
        in_specs=[SMEM, VMEM, VMEM, VMEM],
        out_specs=VMEM,
        out_shape=pltpu.VMEM((blocks, 2, ny, half), BF16),
        name="ymath",
    )(high, near(row_in), near(first_y), near(second_y))
    y_back = exchange(y_term, "z")
    z_back = exchange(z_term, ("x", "l", "c"))
    y_other = partner(y_back[:, 1])
    out = pl.pallas_call(
        final_kernel,
        in_specs=[SMEM] + [VMEM] * 4,
        out_specs=VMEM,
        out_shape=jax.ShapeDtypeStruct((ny, nz, nx), F32),
        scratch_shapes=[pltpu.VMEM((2, ny * nz, LANES), F32)],
        name="last",
    )(high, near(base), near(y_back), near(y_other), near(z_back.reshape(ny, 2, nz, half)))
    return out[None]


def solution(mesh):
    parts = Mesh(mesh.devices.reshape(8, 2, 4, 4, 2), ("z", "h", "x", "l", "c"))
    pencil = P(None, ("z", "h"), ("x", "l", "c"), None)
    return jax.shard_map(
        body,
        mesh=parts,
        in_specs=(pencil, pencil, P(), P(), P(), P(), P(), P()),
        out_specs=pencil,
        check_vma=False,
    )
```

```python
import jax
import jax.numpy as jnp
from jax import lax
from jax.experimental import pallas as pl
from jax.experimental.pallas import tpu as pltpu
from jax.sharding import Mesh
from jax.sharding import PartitionSpec as P


LANES = 128
VMEM = pl.BlockSpec(memory_space=pltpu.VMEM)
SMEM = pl.BlockSpec(memory_space=pltpu.SMEM)
BF16, F32 = jnp.bfloat16, jnp.float32


def component(shape, index):
    return pl.BlockSpec((None,) + shape[1:], lambda i: (index,) + (0,) * (len(shape) - 1))


def near(array):
    return pltpu.with_memory_space_constraint(array, pltpu.VMEM)


def dot(a, b, side):
    return lax.dot_general(a, b, (((1,), (side,)), ((), ())), preferred_element_type=F32)


def term_of(s, c, first, second, product):
    flux = (c * s.astype(F32)).astype(BF16)
    return -0.5 * (c * product(first, s) + product(first, flux)) + 0.5 * product(second, s)


def pack_kernel(s_ref, v_ref, w_ref, row_ref, col_ref, s32, v32):
    ny, nz, nx = s_ref.shape
    half = nx // 2
    for t in range(nx // LANES):
        h, at = divmod(t * LANES, half)
        lanes = slice(t * LANES, (t + 1) * LANES)
        to = slice(at, at + LANES)
        s = s_ref[:, :, lanes]
        s32[t] = s.reshape(ny * nz, LANES)
        v32[t] = v_ref[:, :, lanes].astype(F32).reshape(ny * nz, LANES)
        col_ref[:, h, 0, :, to] = s.astype(BF16)
        col_ref[:, h, 1, :, to] = w_ref[:, :, lanes]
        for z in range(nz):
            row_ref[z, 0, :, lanes] = s32[t, pl.ds(z, ny, stride=nz), :].astype(BF16)
            row_ref[z, 1, :, lanes] = v32[t, pl.ds(z, ny, stride=nz), :].astype(BF16)


def flux_kernel(r_ref, out_ref):
    s = r_ref[:, 0]
    out_ref[0] = s
    out_ref[1] = (r_ref[:, 1].astype(F32) * s.astype(F32)).astype(BF16)


def x_kernel(s_ref, u_ref, first_ref, second_ref, out_ref):
    ny, nz, nx = s_ref.shape
    s = s_ref[...].reshape(ny * nz, nx)
    u = u_ref[...].astype(F32).reshape(ny * nz, nx)
    term = term_of(s.astype(BF16), u, first_ref[...], second_ref[...], lambda m, f: dot(f, m, 1))
    out_ref[...] = (s + 0.5 * term).reshape(ny, nz, nx)


def y_kernel(high_ref, r_ref, own_ref, other_ref, first_ref, second_ref, out_ref, lines):
    _, blocks, depth, lanes = own_ref.shape
    high = high_ref[0]
    length = 2 * blocks * depth
    lines[:, :, high] = own_ref[...]
    lines[:, :, 1 - high] = other_ref[...]
    s = lines[0].reshape(length, lanes)
    flux = lines[1].reshape(length, lanes)
    first = first_ref[:, high].reshape(blocks * depth, length)
    second = second_ref[:, high].reshape(blocks * depth, length)
    c = r_ref[:, 1].reshape(blocks * depth, lanes).astype(F32)
    term = -0.5 * (c * dot(first, s, 0) + dot(first, flux, 0)) + 0.5 * dot(second, s, 0)
    out_ref[...] = term.astype(BF16).reshape(blocks, depth, lanes)


def z_kernel(r_ref, first_ref, second_ref, out_ref):
    blocks, _, depth, lanes = r_ref.shape
    s = r_ref[:, 0].reshape(blocks * depth, lanes)
    c = r_ref[:, 1].reshape(blocks * depth, lanes).astype(F32)
    term = term_of(s, c, first_ref[...], second_ref[...], lambda m, f: dot(m, f, 0))
    out_ref[...] = term.astype(BF16).reshape(blocks, depth, lanes)


def final_kernel(base_ref, y_ref, z_ref, out_ref, y32):
    ny, nz, nx = base_ref.shape
    half = nx // 2
    for t in range(nx // LANES):
        h, at = divmod(t * LANES, half)
        lanes = slice(t * LANES, (t + 1) * LANES)
        of = slice(at, at + LANES)
        for z in range(nz):
            y32[t, pl.ds(z, ny, stride=nz), :] = y_ref[z, :, lanes].astype(F32)
        y = y32[t].reshape(ny, nz, LANES)
        out_ref[:, :, lanes] = base_ref[:, :, lanes] + 0.5 * (y + z_ref[:, h, :, of].astype(F32))


def body(scalars, velocity, first_x, second_x, first_y, second_y, first_z, second_z):
    _, ny, nz, nx = scalars.shape
    half = nx // 2
    blocks = lax.axis_size("z")
    cols = lax.axis_size("x") * lax.axis_size("l") * lax.axis_size("c")
    high = lax.axis_index("h").reshape(1)
    s = scalars[0]
    whole = pl.BlockSpec((ny, nz, nx), lambda i: (0, 0, 0))

    def partner(array):
        return lax.ppermute(array, "h", [(0, 1), (1, 0)])

    def exchange(array, axes):
        return lax.all_to_all(array, axes, split_axis=0, concat_axis=0, tiled=True)

    def rows_split(matrix):
        return near(matrix.reshape(blocks, 2, ny, matrix.shape[1]))

    row_send, col_send = pl.pallas_call(
        pack_kernel,
        grid=(1,),
        in_specs=[whole, component(velocity.shape, 1), component(velocity.shape, 2)],
        out_specs=[VMEM] * 2,
        out_shape=[pltpu.VMEM((blocks, 2, ny, nx), BF16), pltpu.VMEM((ny, 2, 2, nz, half), BF16)],
        scratch_shapes=[pltpu.VMEM((nx // LANES, ny * nz, LANES), F32)] * 2,
        name="pack",
    )(s, velocity, velocity)
    row_in = near(exchange(row_send, "z"))
    col_in = exchange(col_send.reshape(cols, 2, nz, half), ("x", "l", "c"))
    own = pl.pallas_call(
        flux_kernel,
        in_specs=[VMEM],
        out_specs=VMEM,
        out_shape=pltpu.VMEM((2, blocks, ny, nx), BF16),
        name="flux",
    )(row_in)
    other = partner(own)
    base = pl.pallas_call(
        x_kernel,
        grid=(1,),
        in_specs=[whole, component(velocity.shape, 0), VMEM, VMEM],
        out_specs=VMEM,
        out_shape=pltpu.VMEM((ny, nz, nx), F32),
        name="xmath",
    )(s, velocity, near(first_x), near(second_x))
    z_term = pl.pallas_call(
        z_kernel,
        in_specs=[VMEM] * 3,
        out_specs=VMEM,
        out_shape=pltpu.VMEM((cols, nz, half), BF16),
        name="zmath",
    )(near(col_in), near(first_z), near(second_z))
    z_back = exchange(z_term, ("x", "l", "c"))
    y_term = pl.pallas_call(
        y_kernel,
        in_specs=[SMEM] + [VMEM] * 5,
        out_specs=VMEM,
        out_shape=pltpu.VMEM((blocks, ny, nx), BF16),
        scratch_shapes=[pltpu.VMEM((2, blocks, 2, ny, nx), BF16)],
        name="ymath",
    )(high, row_in, near(own), near(other), rows_split(first_y), rows_split(second_y))
    y_back = exchange(y_term, "z")
    out = pl.pallas_call(
        final_kernel,
        in_specs=[VMEM] * 3,
        out_specs=VMEM,
        out_shape=jax.ShapeDtypeStruct((ny, nz, nx), F32),
        scratch_shapes=[pltpu.VMEM((nx // LANES, ny * nz, LANES), F32)],
        name="last",
    )(near(base), near(y_back), near(z_back.reshape(ny, 2, nz, half)))
    return out[None]


def solution(mesh):
    parts = Mesh(mesh.devices.reshape(8, 2, 4, 4, 2), ("z", "h", "x", "l", "c"))
    pencil = P(None, ("z", "h"), ("x", "l", "c"), None)
    return jax.shard_map(
        body,
        mesh=parts,
        in_specs=(pencil, pencil, P(), P(), P(), P(), P(), P()),
        out_specs=pencil,
        check_vma=False,
    )
```

```python
import jax
import jax.numpy as jnp
from jax import lax
from jax.experimental import pallas as pl
from jax.experimental.pallas import tpu as pltpu
from jax.sharding import Mesh
from jax.sharding import PartitionSpec as P


LANES = 128
VMEM = pl.BlockSpec(memory_space=pltpu.VMEM)
SMEM = pl.BlockSpec(memory_space=pltpu.SMEM)
BF16, F32 = jnp.bfloat16, jnp.float32


def component(shape, index):
    return pl.BlockSpec((None,) + shape[1:], lambda i: (index,) + (0,) * (len(shape) - 1))


def near(array):
    return pltpu.with_memory_space_constraint(array, pltpu.VMEM)


def dot(a, b, side):
    return lax.dot_general(a, b, (((1,), (side,)), ((), ())), preferred_element_type=F32)


def term_of(s, c, first, second, product):
    flux = (c * s.astype(F32)).astype(BF16)
    return -0.5 * (c * product(first, s) + product(first, flux)) + 0.5 * product(second, s)


def pack_kernel(low_ref, s_ref, v_ref, w_ref, row_ref, *rest):
    pieces, (s32, v32) = rest[:-2], rest[-2:]
    ny, nz, nx = s_ref.shape
    half = nx // 2
    group = ny // len(pieces)
    low = low_ref[0]
    for j, piece in enumerate(pieces):
        for q in range(group):
            y = (low ^ j) * group + q
            for h in range(2):
                lanes = slice(h * half, (h + 1) * half)
                piece[2 * q + h, 0] = s_ref[y, :, lanes].astype(BF16)
                piece[2 * q + h, 1] = w_ref[y, :, lanes]
    for t in range(nx // LANES):
        lanes = slice(t * LANES, (t + 1) * LANES)
        s32[t] = s_ref[:, :, lanes].reshape(ny * nz, LANES)
        v32[t] = v_ref[:, :, lanes].astype(F32).reshape(ny * nz, LANES)
        for z in range(nz):
            row_ref[z, 0, :, lanes] = s32[t, pl.ds(z, ny, stride=nz), :].astype(BF16)
            row_ref[z, 1, :, lanes] = v32[t, pl.ds(z, ny, stride=nz), :].astype(BF16)


def join_kernel(*refs):
    for j, piece in enumerate(refs[:-1]):
        refs[-1][:, j] = piece[...]


def flux_kernel(r_ref, out_ref):
    s = r_ref[:, 0]
    out_ref[0] = s
    out_ref[1] = (r_ref[:, 1].astype(F32) * s.astype(F32)).astype(BF16)


def x_kernel(s_ref, u_ref, first_ref, second_ref, out_ref):
    ny, nz, nx = s_ref.shape
    s = s_ref[...].reshape(ny * nz, nx)
    u = u_ref[...].astype(F32).reshape(ny * nz, nx)
    term = term_of(s.astype(BF16), u, first_ref[...], second_ref[...], lambda m, f: dot(f, m, 1))
    out_ref[...] = (s + 0.5 * term).reshape(ny, nz, nx)


def y_kernel(high_ref, r_ref, own_ref, other_ref, first_ref, second_ref, out_ref, lines):
    _, blocks, depth, lanes = own_ref.shape
    high = high_ref[0]
    length = 2 * blocks * depth
    lines[:, :, high] = own_ref[...]
    lines[:, :, 1 - high] = other_ref[...]
    s = lines[0].reshape(length, lanes)
    flux = lines[1].reshape(length, lanes)
    first = first_ref[:, high].reshape(blocks * depth, length)
    second = second_ref[:, high].reshape(blocks * depth, length)
    c = r_ref[:, 1].reshape(blocks * depth, lanes).astype(F32)
    term = -0.5 * (c * dot(first, s, 0) + dot(first, flux, 0)) + 0.5 * dot(second, s, 0)
    out_ref[...] = term.astype(BF16).reshape(blocks, depth, lanes)


def z_kernel(low_ref, r_ref, first_ref, second_ref, out_ref, lines, terms):
    _, nx_blocks, lows, cores, depth, lanes = lines.shape
    low = low_ref[0]
    length = nx_blocks * lows * cores * depth
    for f in range(2):
        for x in range(nx_blocks):
            for j in range(lows):
                for c in range(cores):
                    lines[f, x, low ^ j, c] = r_ref[x * cores + c, j, f]
    s = lines[0].reshape(length, lanes)
    c = lines[1].reshape(length, lanes).astype(F32)
    term = term_of(s, c, first_ref[...], second_ref[...], lambda m, f: dot(m, f, 0))
    terms[...] = term.astype(BF16).reshape(terms.shape)
    for x in range(nx_blocks):
        for j in range(lows):
            for c in range(cores):
                out_ref[x * cores + c, j] = terms[x, low ^ j, c]


def final_kernel(low_ref, base_ref, y_ref, own_ref, *rest):
    others, (out_ref, y32) = rest[:-2], rest[-2:]
    ny, nz, nx = base_ref.shape
    half = nx // 2
    group = ny // (1 + len(others))
    low = low_ref[0]
    for t in range(nx // LANES):
        h, at = divmod(t * LANES, half)
        lanes = slice(t * LANES, (t + 1) * LANES)
        of = slice(at, at + LANES)
        for z in range(nz):
            y32[t, pl.ds(z, ny, stride=nz), :] = y_ref[z, :, lanes].astype(F32)
        for j in range(1 + len(others)):
            for q in range(group):
                y = (low ^ j) * group + q
                z_term = others[j - 1][2 * q + h, :, of] if j else own_ref[2 * q + h, 0, :, of]
                y_term = y32[t, pl.ds(pl.multiple_of(y * nz, nz), nz), :]
                out_ref[y, :, lanes] = base_ref[y, :, lanes] + 0.5 * (y_term + z_term.astype(F32))


def body(scalars, velocity, first_x, second_x, first_y, second_y, first_z, second_z):
    _, ny, nz, nx = scalars.shape
    half = nx // 2
    blocks, lows, cores = lax.axis_size("z"), lax.axis_size("l"), lax.axis_size("c")
    peers = lax.axis_size("x") * cores
    high = lax.axis_index("h").reshape(1)
    low = lax.axis_index("l").reshape(1)
    s = scalars[0]
    whole = pl.BlockSpec((ny, nz, nx), lambda i: (0, 0, 0))

    def swap(array, axis, j):
        return lax.ppermute(array, axis, [(i, i ^ j) for i in range(lax.axis_size(axis))])

    def exchange(array, axes):
        return lax.all_to_all(array, axes, split_axis=0, concat_axis=0, tiled=True)

    def rows_split(matrix):
        return near(matrix.reshape(blocks, 2, ny, matrix.shape[1]))

    row_send, keep, *give = pl.pallas_call(
        pack_kernel,
        grid=(1,),
        in_specs=[SMEM, whole, component(velocity.shape, 1), component(velocity.shape, 2)],
        out_specs=[VMEM] * (1 + lows),
        out_shape=[pltpu.VMEM((blocks, 2, ny, nx), BF16)] + [pltpu.VMEM((peers, 2, nz, half), BF16)] * lows,
        scratch_shapes=[pltpu.VMEM((nx // LANES, ny * nz, LANES), F32)] * 2,
        name="pack",
    )(low, s, velocity, velocity)
    row_in = near(exchange(row_send, "z"))
    got = []
    for j, piece in enumerate(give, 1):
        got.append(near(swap(piece, "l", j)))
    col_send = pl.pallas_call(
        join_kernel,
        in_specs=[VMEM] * lows,
        out_specs=VMEM,
        out_shape=pltpu.VMEM((peers, lows, 2, nz, half), BF16),
        name="join",
    )(near(keep), *got)
    col_in = exchange(col_send, ("x", "c"))
    own = pl.pallas_call(
        flux_kernel,
        in_specs=[VMEM],
        out_specs=VMEM,
        out_shape=pltpu.VMEM((2, blocks, ny, nx), BF16),
        name="flux",
    )(row_in)
    other = swap(own, "h", 1)
    base = pl.pallas_call(
        x_kernel,
        grid=(1,),
        in_specs=[whole, component(velocity.shape, 0), VMEM, VMEM],
        out_specs=VMEM,
        out_shape=pltpu.VMEM((ny, nz, nx), F32),
        name="xmath",
    )(s, velocity, near(first_x), near(second_x))
    z_term = pl.pallas_call(
        z_kernel,
        in_specs=[SMEM] + [VMEM] * 3,
        out_specs=VMEM,
        out_shape=pltpu.VMEM((peers, lows, nz, half), BF16),
        scratch_shapes=[
            pltpu.VMEM((2, peers // cores, lows, cores, nz, half), BF16),
            pltpu.VMEM((peers // cores, lows, cores, nz, half), BF16),
        ],
        name="zmath",
    )(low, near(col_in), near(first_z), near(second_z))
    z_back = exchange(z_term, ("x", "c"))
    y_term = pl.pallas_call(
        y_kernel,
        in_specs=[SMEM] + [VMEM] * 5,
        out_specs=VMEM,
        out_shape=pltpu.VMEM((blocks, ny, nx), BF16),
        scratch_shapes=[pltpu.VMEM((2, blocks, 2, ny, nx), BF16)],
        name="ymath",
    )(high, row_in, near(own), near(other), rows_split(first_y), rows_split(second_y))
    y_back = exchange(y_term, "z")
    returned = []
    for j in range(1, lows):
        returned.append(near(swap(z_back[:, j], "l", j)))
    out = pl.pallas_call(
        final_kernel,
        in_specs=[SMEM] + [VMEM] * (2 + lows),
        out_specs=VMEM,
        out_shape=jax.ShapeDtypeStruct((ny, nz, nx), F32),
        scratch_shapes=[pltpu.VMEM((nx // LANES, ny * nz, LANES), F32)],
        name="last",
    )(low, near(base), near(y_back), near(z_back), *returned)
    return out[None]


def solution(mesh):
    parts = Mesh(mesh.devices.reshape(8, 2, 4, 4, 2), ("z", "h", "x", "l", "c"))
    pencil = P(None, ("z", "h"), ("x", "l", "c"), None)
    return jax.shard_map(
        body,
        mesh=parts,
        in_specs=(pencil, pencil, P(), P(), P(), P(), P(), P()),
        out_specs=pencil,
        check_vma=False,
    )
```

```python
import jax
import jax.numpy as jnp
from jax import lax
from jax.experimental import pallas as pl
from jax.experimental.pallas import tpu as pltpu
from jax.sharding import Mesh
from jax.sharding import PartitionSpec as P


LANES = 128
VMEM = pl.BlockSpec(memory_space=pltpu.VMEM)
SMEM = pl.BlockSpec(memory_space=pltpu.SMEM)
BF16, F32 = jnp.bfloat16, jnp.float32


def component(shape, index):
    return pl.BlockSpec((None,) + shape[1:], lambda i: (index,) + (0,) * (len(shape) - 1))


def near(array):
    return pltpu.with_memory_space_constraint(array, pltpu.VMEM)


def dot(a, b, side):
    return lax.dot_general(a, b, (((1,), (side,)), ((), ())), preferred_element_type=F32)


def term_of(s, c, first, second, product):
    flux = (c * s.astype(F32)).astype(BF16)
    return -0.5 * (c * product(first, s) + product(first, flux)) + 0.5 * product(second, s)


def pack_kernel(low_ref, s_ref, v_ref, w_ref, row_ref, *rest):
    pieces, (s32, v32) = rest[:-2], rest[-2:]
    ny, nz, nx = s_ref.shape
    half = nx // 2
    group = ny // len(pieces)
    low = low_ref[0]
    for j, piece in enumerate(pieces):
        for q in range(group):
            y = (low ^ j) * group + q
            for h in range(2):
                lanes = slice(h * half, (h + 1) * half)
                piece[2 * q + h, 0] = s_ref[y, :, lanes].astype(BF16)
                piece[2 * q + h, 1] = w_ref[y, :, lanes]
    for t in range(nx // LANES):
        lanes = slice(t * LANES, (t + 1) * LANES)
        s32[t] = s_ref[:, :, lanes].reshape(ny * nz, LANES)
        v32[t] = v_ref[:, :, lanes].astype(F32).reshape(ny * nz, LANES)
        for z in range(nz):
            row_ref[z, 0, :, lanes] = s32[t, pl.ds(z, ny, stride=nz), :].astype(BF16)
            row_ref[z, 1, :, lanes] = v32[t, pl.ds(z, ny, stride=nz), :].astype(BF16)


def join_kernel(*refs):
    for j, piece in enumerate(refs[:-1]):
        refs[-1][:, j] = piece[...]


def flux_kernel(r_ref, out_ref):
    s = r_ref[:, 0]
    out_ref[0] = s
    out_ref[1] = (r_ref[:, 1].astype(F32) * s.astype(F32)).astype(BF16)


def x_kernel(s_ref, u_ref, first_ref, second_ref, out_ref):
    ny, nz, nx = s_ref.shape
    s = s_ref[...].reshape(ny * nz, nx)
    u = u_ref[...].astype(F32).reshape(ny * nz, nx)
    term = term_of(s.astype(BF16), u, first_ref[...], second_ref[...], lambda m, f: dot(f, m, 1))
    out_ref[...] = (s + 0.5 * term).reshape(ny, nz, nx)


def y_kernel(high_ref, r_ref, own_ref, other_ref, first_ref, second_ref, out_ref, lines):
    _, blocks, depth, lanes = own_ref.shape
    high = high_ref[0]
    length = 2 * blocks * depth
    lines[:, :, high] = own_ref[...]
    lines[:, :, 1 - high] = other_ref[...]
    s = lines[0].reshape(length, lanes)
    flux = lines[1].reshape(length, lanes)
    first = first_ref[:, high].reshape(blocks * depth, length)
    second = second_ref[:, high].reshape(blocks * depth, length)
    c = r_ref[:, 1].reshape(blocks * depth, lanes).astype(F32)
    term = -0.5 * (c * dot(first, s, 0) + dot(first, flux, 0)) + 0.5 * dot(second, s, 0)
    out_ref[...] = term.astype(BF16).reshape(blocks, depth, lanes)


def z_kernel(low_ref, r_ref, first_ref, second_ref, out_ref, lines, terms):
    _, nx_blocks, lows, cores, depth, lanes = lines.shape
    low = low_ref[0]
    length = nx_blocks * lows * cores * depth
    for f in range(2):
        for x in range(nx_blocks):
            for j in range(lows):
                for c in range(cores):
                    lines[f, x, low ^ j, c] = r_ref[x * cores + c, j, f]
    s = lines[0].reshape(length, lanes)
    c = lines[1].reshape(length, lanes).astype(F32)
    term = term_of(s, c, first_ref[...], second_ref[...], lambda m, f: dot(m, f, 0))
    terms[...] = term.astype(BF16).reshape(terms.shape)
    for x in range(nx_blocks):
        for j in range(lows):
            for c in range(cores):
                out_ref[x * cores + c, j] = terms[x, low ^ j, c]


def final_kernel(low_ref, base_ref, y_ref, own_ref, *rest):
    others, (out_ref, y32) = rest[:-2], rest[-2:]
    ny, nz, nx = base_ref.shape
    half = nx // 2
    group = ny // (1 + len(others))
    low = low_ref[0]
    for t in range(nx // LANES):
        h, at = divmod(t * LANES, half)
        lanes = slice(t * LANES, (t + 1) * LANES)
        of = slice(at, at + LANES)
        for z in range(nz):
            y32[t, pl.ds(z, ny, stride=nz), :] = y_ref[z, :, lanes].astype(F32)
        for j in range(1 + len(others)):
            for q in range(group):
                y = (low ^ j) * group + q
                z_term = others[j - 1][2 * q + h, :, of] if j else own_ref[2 * q + h, 0, :, of]
                y_term = y32[t, pl.ds(pl.multiple_of(y * nz, nz), nz), :]
                out_ref[y, :, lanes] = base_ref[y, :, lanes] + 0.5 * (y_term + z_term.astype(F32))


def body(scalars, velocity, first_x, second_x, first_y, second_y, first_z, second_z):
    _, ny, nz, nx = scalars.shape
    half = nx // 2
    blocks, lows = lax.axis_size("z"), lax.axis_size("m")
    cores = lax.axis_size("l") * lax.axis_size("c")
    peers = lax.axis_size("x") * cores
    high = lax.axis_index("h").reshape(1)
    low = lax.axis_index("m").reshape(1)
    s = scalars[0]
    whole = pl.BlockSpec((ny, nz, nx), lambda i: (0, 0, 0))

    def swap(array, axis, j):
        return lax.ppermute(array, axis, [(i, i ^ j) for i in range(lax.axis_size(axis))])

    def exchange(array, axes):
        return lax.all_to_all(array, axes, split_axis=0, concat_axis=0, tiled=True)

    def rows_split(matrix):
        return near(matrix.reshape(blocks, 2, ny, matrix.shape[1]))

    row_send, keep, *give = pl.pallas_call(
        pack_kernel,
        grid=(1,),
        in_specs=[SMEM, whole, component(velocity.shape, 1), component(velocity.shape, 2)],
        out_specs=[VMEM] * (1 + lows),
        out_shape=[pltpu.VMEM((blocks, 2, ny, nx), BF16)] + [pltpu.VMEM((peers, 2, nz, half), BF16)] * lows,
        scratch_shapes=[pltpu.VMEM((nx // LANES, ny * nz, LANES), F32)] * 2,
        name="pack",
    )(low, s, velocity, velocity)
    row_in = near(exchange(row_send, "z"))
    got = []
    for j, piece in enumerate(give, 1):
        got.append(near(swap(piece, "m", j)))
    col_send = pl.pallas_call(
        join_kernel,
        in_specs=[VMEM] * lows,
        out_specs=VMEM,
        out_shape=pltpu.VMEM((peers, lows, 2, nz, half), BF16),
        name="join",
    )(near(keep), *got)
    col_in = exchange(col_send, ("x", "l", "c"))
    own = pl.pallas_call(
        flux_kernel,
        in_specs=[VMEM],
        out_specs=VMEM,
        out_shape=pltpu.VMEM((2, blocks, ny, nx), BF16),
        name="flux",
    )(row_in)
    other = swap(own, "h", 1)
    base = pl.pallas_call(
        x_kernel,
        grid=(1,),
        in_specs=[whole, component(velocity.shape, 0), VMEM, VMEM],
        out_specs=VMEM,
        out_shape=pltpu.VMEM((ny, nz, nx), F32),
        name="xmath",
    )(s, velocity, near(first_x), near(second_x))
    z_term = pl.pallas_call(
        z_kernel,
        in_specs=[SMEM] + [VMEM] * 3,
        out_specs=VMEM,
        out_shape=pltpu.VMEM((peers, lows, nz, half), BF16),
        scratch_shapes=[
            pltpu.VMEM((2, peers // cores, lows, cores, nz, half), BF16),
            pltpu.VMEM((peers // cores, lows, cores, nz, half), BF16),
        ],
        name="zmath",
    )(low, near(col_in), near(first_z), near(second_z))
    z_back = exchange(z_term, ("x", "l", "c"))
    y_term = pl.pallas_call(
        y_kernel,
        in_specs=[SMEM] + [VMEM] * 5,
        out_specs=VMEM,
        out_shape=pltpu.VMEM((blocks, ny, nx), BF16),
        scratch_shapes=[pltpu.VMEM((2, blocks, 2, ny, nx), BF16)],
        name="ymath",
    )(high, row_in, near(own), near(other), rows_split(first_y), rows_split(second_y))
    y_back = exchange(y_term, "z")
    returned = []
    for j in range(1, lows):
        returned.append(near(swap(z_back[:, j], "m", j)))
    out = pl.pallas_call(
        final_kernel,
        in_specs=[SMEM] + [VMEM] * (2 + lows),
        out_specs=VMEM,
        out_shape=jax.ShapeDtypeStruct((ny, nz, nx), F32),
        scratch_shapes=[pltpu.VMEM((nx // LANES, ny * nz, LANES), F32)],
        name="last",
    )(low, near(base), near(y_back), near(z_back), *returned)
    return out[None]


def solution(mesh):
    parts = Mesh(mesh.devices.reshape(8, 2, 4, 2, 2, 2), ("z", "h", "x", "m", "l", "c"))
    pencil = P(None, ("z", "h"), ("x", "m", "l", "c"), None)
    return jax.shard_map(
        body,
        mesh=parts,
        in_specs=(pencil, pencil, P(), P(), P(), P(), P(), P()),
        out_specs=pencil,
        check_vma=False,
    )
```

```python
import jax
import jax.numpy as jnp
from jax import lax
from jax.experimental import pallas as pl
from jax.experimental.pallas import tpu as pltpu
from jax.sharding import Mesh
from jax.sharding import PartitionSpec as P


LANES = 128
VMEM = pl.BlockSpec(memory_space=pltpu.VMEM)
SMEM = pl.BlockSpec(memory_space=pltpu.SMEM)
BF16, F32 = jnp.bfloat16, jnp.float32


def component(shape, index):
    return pl.BlockSpec((None,) + shape[1:], lambda i: (index,) + (0,) * (len(shape) - 1))


def near(array):
    return pltpu.with_memory_space_constraint(array, pltpu.VMEM)


def dot(a, b, side):
    return lax.dot_general(a, b, (((1,), (side,)), ((), ())), preferred_element_type=F32)


def term_of(s, c, first, second, product):
    flux = (c * s.astype(F32)).astype(BF16)
    return -0.5 * (c * product(first, s) + product(first, flux)) + 0.5 * product(second, s)


def pack_kernel(low_ref, s_ref, v_ref, w_ref, row_ref, *rest):
    pieces, (s32, v32) = rest[:-2], rest[-2:]
    ny, nz, nx = s_ref.shape
    half = nx // 2
    group = ny // len(pieces)
    low = low_ref[0]
    for j, piece in enumerate(pieces):
        for q in range(group):
            y = (low ^ j) * group + q
            for h in range(2):
                lanes = slice(h * half, (h + 1) * half)
                piece[2 * q + h, 0] = s_ref[y, :, lanes].astype(BF16)
                piece[2 * q + h, 1] = w_ref[y, :, lanes]
    for t in range(nx // LANES):
        lanes = slice(t * LANES, (t + 1) * LANES)
        s32[t] = s_ref[:, :, lanes].reshape(ny * nz, LANES)
        v32[t] = v_ref[:, :, lanes].astype(F32).reshape(ny * nz, LANES)
        for z in range(nz):
            row_ref[z, 0, :, lanes] = s32[t, pl.ds(z, ny, stride=nz), :].astype(BF16)
            row_ref[z, 1, :, lanes] = v32[t, pl.ds(z, ny, stride=nz), :].astype(BF16)


def join_kernel(*refs):
    for j, piece in enumerate(refs[:-1]):
        refs[-1][:, j] = piece[...]


def flux_kernel(r_ref, out_ref):
    s = r_ref[:, 0]
    out_ref[0] = s
    out_ref[1] = (r_ref[:, 1].astype(F32) * s.astype(F32)).astype(BF16)


def x_kernel(s_ref, u_ref, first_ref, second_ref, out_ref):
    ny, nz, nx = s_ref.shape
    s = s_ref[...].reshape(ny * nz, nx)
    u = u_ref[...].astype(F32).reshape(ny * nz, nx)
    term = term_of(s.astype(BF16), u, first_ref[...], second_ref[...], lambda m, f: dot(f, m, 1))
    out_ref[...] = (s + 0.5 * term).reshape(ny, nz, nx)


def rows_kernel(high_ref, first_ref, second_ref, out_ref):
    high = high_ref[0]
    out_ref[0] = first_ref[:, high]
    out_ref[1] = second_ref[:, high]


def y_kernel(high_ref, r_ref, own_ref, other_ref, rows_ref, out_ref, lines):
    _, blocks, depth, lanes = own_ref.shape
    high = high_ref[0]
    length = 2 * blocks * depth
    lines[:, :, high] = own_ref[...]
    lines[:, :, 1 - high] = other_ref[...]
    s = lines[0].reshape(length, lanes)
    flux = lines[1].reshape(length, lanes)
    first = rows_ref[0].reshape(blocks * depth, length)
    second = rows_ref[1].reshape(blocks * depth, length)
    c = r_ref[:, 1].reshape(blocks * depth, lanes).astype(F32)
    term = -0.5 * (c * dot(first, s, 0) + dot(first, flux, 0)) + 0.5 * dot(second, s, 0)
    out_ref[...] = term.astype(BF16).reshape(blocks, depth, lanes)


def z_kernel(low_ref, r_ref, first_ref, second_ref, out_ref, lines):
    _, nx_blocks, lows, cores, depth, lanes = lines.shape
    low = low_ref[0]
    length = nx_blocks * lows * cores * depth
    for f in range(2):
        for x in range(nx_blocks):
            for j in range(lows):
                for c in range(cores):
                    lines[f, x, low ^ j, c] = r_ref[x * cores + c, j, f]
    s = lines[0].reshape(length, lanes)
    c = lines[1].reshape(length, lanes).astype(F32)
    term = term_of(s, c, first_ref[...], second_ref[...], lambda m, f: dot(m, f, 0))
    out_ref[...] = term.astype(BF16).reshape(out_ref.shape)


def final_kernel(base_ref, y_ref, z_ref, out_ref, y32):
    ny, nz, nx = base_ref.shape
    nx_blocks, lows, cores, _, half = z_ref.shape
    for t in range(nx // LANES):
        h, at = divmod(t * LANES, half)
        lanes = slice(t * LANES, (t + 1) * LANES)
        of = slice(at, at + LANES)
        for z in range(nz):
            y32[t, pl.ds(z, ny, stride=nz), :] = y_ref[z, :, lanes].astype(F32)
        for x in range(nx_blocks):
            for j in range(lows):
                for c in range(h, cores, 2):
                    y = (j * nx_blocks + x) * (cores // 2) + c // 2
                    y_term = y32[t, y * nz:(y + 1) * nz, :]
                    z_term = z_ref[x, j, c, :, of].astype(F32)
                    out_ref[y, :, lanes] = base_ref[y, :, lanes] + 0.5 * (y_term + z_term)


def body(scalars, velocity, first_x, second_x, first_y, second_y, first_z, second_z):
    _, ny, nz, nx = scalars.shape
    half = nx // 2
    blocks, lows = lax.axis_size("z"), lax.axis_size("m")
    cores = lax.axis_size("l") * lax.axis_size("c")
    peers = lax.axis_size("x") * cores
    high = lax.axis_index("h").reshape(1)
    low = lax.axis_index("m").reshape(1)
    s = scalars[0]
    whole = pl.BlockSpec((ny, nz, nx), lambda i: (0, 0, 0))

    def swap(array, axis, j):
        return lax.ppermute(array, axis, [(i, i ^ j) for i in range(lax.axis_size(axis))])

    def exchange(array, axes):
        return lax.all_to_all(array, axes, split_axis=0, concat_axis=0, tiled=True)

    def rows_split(matrix):
        return near(matrix.reshape(blocks, 2, ny, matrix.shape[1]))

    row_send, keep, *give = pl.pallas_call(
        pack_kernel,
        grid=(1,),
        in_specs=[SMEM, whole, component(velocity.shape, 1), component(velocity.shape, 2)],
        out_specs=[VMEM] * (1 + lows),
        out_shape=[pltpu.VMEM((blocks, 2, ny, nx), BF16)] + [pltpu.VMEM((peers, 2, nz, half), BF16)] * lows,
        scratch_shapes=[pltpu.VMEM((nx // LANES, ny * nz, LANES), F32)] * 2,
        name="pack",
    )(low, s, velocity, velocity)
    row_in = near(exchange(row_send, "z"))
    got = []
    for j, piece in enumerate(give, 1):
        got.append(near(swap(piece, "m", j)))
    col_send = pl.pallas_call(
        join_kernel,
        in_specs=[VMEM] * lows,
        out_specs=VMEM,
        out_shape=pltpu.VMEM((peers, lows, 2, nz, half), BF16),
        name="join",
    )(near(keep), *got)
    col_in = exchange(col_send, ("x", "l", "c"))
    own = pl.pallas_call(
        flux_kernel,
        in_specs=[VMEM],
        out_specs=VMEM,
        out_shape=pltpu.VMEM((2, blocks, ny, nx), BF16),
        name="flux",
    )(row_in)
    other = swap(own, "h", 1)
    base = pl.pallas_call(
        x_kernel,
        grid=(1,),
        in_specs=[whole, component(velocity.shape, 0), VMEM, VMEM],
        out_specs=VMEM,
        out_shape=pltpu.VMEM((ny, nz, nx), F32),
        name="xmath",
    )(s, velocity, near(first_x), near(second_x))
    rows = pl.pallas_call(
        rows_kernel,
        in_specs=[SMEM] + [VMEM] * 2,
        out_specs=VMEM,
        out_shape=pltpu.VMEM((2, blocks, ny, first_y.shape[1]), BF16),
        name="rows",
    )(high, rows_split(first_y), rows_split(second_y))
    z_term = pl.pallas_call(
        z_kernel,
        in_specs=[SMEM] + [VMEM] * 3,
        out_specs=VMEM,
        out_shape=pltpu.VMEM((peers * lows, nz, half), BF16),
        scratch_shapes=[pltpu.VMEM((2, peers // cores, lows, cores, nz, half), BF16)],
        name="zmath",
    )(low, near(col_in), near(first_z), near(second_z))
    z_back = exchange(z_term, ("x", "m", "l", "c"))
    y_term = pl.pallas_call(
        y_kernel,
        in_specs=[SMEM] + [VMEM] * 4,
        out_specs=VMEM,
        out_shape=pltpu.VMEM((blocks, ny, nx), BF16),
        scratch_shapes=[pltpu.VMEM((2, blocks, 2, ny, nx), BF16)],
        name="ymath",
    )(high, row_in, near(own), near(other), near(rows))
    y_back = exchange(y_term, "z")
    out = pl.pallas_call(
        final_kernel,
        in_specs=[VMEM] * 3,
        out_specs=VMEM,
        out_shape=jax.ShapeDtypeStruct((ny, nz, nx), F32),
        scratch_shapes=[pltpu.VMEM((nx // LANES, ny * nz, LANES), F32)],
        name="last",
    )(near(base), near(y_back), near(z_back.reshape(peers // cores, lows, cores, nz, half)))
    return out[None]


def solution(mesh):
    parts = Mesh(mesh.devices.reshape(8, 2, 4, 2, 2, 2), ("z", "h", "x", "m", "l", "c"))
    pencil = P(None, ("z", "h"), ("x", "m", "l", "c"), None)
    return jax.shard_map(
        body,
        mesh=parts,
        in_specs=(pencil, pencil, P(), P(), P(), P(), P(), P()),
        out_specs=pencil,
        check_vma=False,
    )
```

```python
import jax
import jax.numpy as jnp
from jax import lax
from jax.experimental import pallas as pl
from jax.experimental.pallas import tpu as pltpu
from jax.sharding import Mesh
from jax.sharding import PartitionSpec as P


LANES = 128
VMEM = pl.BlockSpec(memory_space=pltpu.VMEM)
SMEM = pl.BlockSpec(memory_space=pltpu.SMEM)
BF16, F32 = jnp.bfloat16, jnp.float32


def component(shape, index):
    return pl.BlockSpec((None,) + shape[1:], lambda i: (index,) + (0,) * (len(shape) - 1))


def near(array):
    return pltpu.with_memory_space_constraint(array, pltpu.VMEM)


def dot(a, b, side):
    return lax.dot_general(a, b, (((1,), (side,)), ((), ())), preferred_element_type=F32)


def term_of(s, c, first, second, product):
    flux = (c * s.astype(F32)).astype(BF16)
    return -0.5 * (c * product(first, s) + product(first, flux)) + 0.5 * product(second, s)


def pack_kernel(s_ref, v_ref, row_ref, s32, v32):
    ny, nz, nx = s_ref.shape
    for t in range(nx // LANES):
        lanes = slice(t * LANES, (t + 1) * LANES)
        s32[t] = s_ref[:, :, lanes].reshape(ny * nz, LANES)
        v32[t] = v_ref[:, :, lanes].astype(F32).reshape(ny * nz, LANES)
        for z in range(nz):
            row_ref[z, 0, :, lanes] = s32[t, pl.ds(z, ny, stride=nz), :].astype(BF16)
            row_ref[z, 1, :, lanes] = v32[t, pl.ds(z, ny, stride=nz), :].astype(BF16)


def pieces_kernel(low_ref, s_ref, w_ref, *pieces):
    ny, _, nx = s_ref.shape
    half = nx // 2
    group = ny // len(pieces)
    low = low_ref[0]
    for j, piece in enumerate(pieces):
        for q in range(group):
            y = (low ^ j) * group + q
            for h in range(2):
                lanes = slice(h * half, (h + 1) * half)
                piece[2 * q + h, 0] = s_ref[y, :, lanes].astype(BF16)
                piece[2 * q + h, 1] = w_ref[y, :, lanes]


def join_kernel(*refs):
    for j, piece in enumerate(refs[:-1]):
        refs[-1][:, j] = piece[...]


def flux_kernel(r_ref, out_ref):
    s = r_ref[:, 0]
    out_ref[0] = s
    out_ref[1] = (r_ref[:, 1].astype(F32) * s.astype(F32)).astype(BF16)


def x_kernel(s_ref, u_ref, first_ref, second_ref, out_ref):
    ny, nz, nx = s_ref.shape
    s = s_ref[...].reshape(ny * nz, nx)
    u = u_ref[...].astype(F32).reshape(ny * nz, nx)
    term = term_of(s.astype(BF16), u, first_ref[...], second_ref[...], lambda m, f: dot(f, m, 1))
    out_ref[...] = (s + 0.5 * term).reshape(ny, nz, nx)


def rows_kernel(high_ref, first_ref, second_ref, out_ref):
    high = high_ref[0]
    out_ref[0] = first_ref[:, high]
    out_ref[1] = second_ref[:, high]


def y_kernel(high_ref, r_ref, own_ref, other_ref, rows_ref, out_ref, lines):
    _, blocks, depth, lanes = own_ref.shape
    high = high_ref[0]
    length = 2 * blocks * depth
    lines[:, :, high] = own_ref[...]
    lines[:, :, 1 - high] = other_ref[...]
    s = lines[0].reshape(length, lanes)
    flux = lines[1].reshape(length, lanes)
    first = rows_ref[0].reshape(blocks * depth, length)
    second = rows_ref[1].reshape(blocks * depth, length)
    c = r_ref[:, 1].reshape(blocks * depth, lanes).astype(F32)
    term = -0.5 * (c * dot(first, s, 0) + dot(first, flux, 0)) + 0.5 * dot(second, s, 0)
    out_ref[...] = term.astype(BF16).reshape(blocks, depth, lanes)


def z_kernel(low_ref, r_ref, first_ref, second_ref, out_ref, lines, terms):
    _, nx_blocks, lows, cores, depth, lanes = lines.shape
    low = low_ref[0]
    length = nx_blocks * lows * cores * depth
    for f in range(2):
        for x in range(nx_blocks):
            for j in range(lows):
                for c in range(cores):
                    lines[f, x, low ^ j, c] = r_ref[x * cores + c, j, f]
    s = lines[0].reshape(length, lanes)
    c = lines[1].reshape(length, lanes).astype(F32)
    term = term_of(s, c, first_ref[...], second_ref[...], lambda m, f: dot(m, f, 0))
    terms[...] = term.astype(BF16).reshape(terms.shape)
    for x in range(nx_blocks):
        for j in range(lows):
            for c in range(cores):
                out_ref[x * cores + c, j] = terms[x, low ^ j, c]


def final_kernel(low_ref, base_ref, y_ref, own_ref, *rest):
    others, (out_ref, y32) = rest[:-2], rest[-2:]
    ny, nz, nx = base_ref.shape
    half = nx // 2
    group = ny // (1 + len(others))
    low = low_ref[0]
    for t in range(nx // LANES):
        h, at = divmod(t * LANES, half)
        lanes = slice(t * LANES, (t + 1) * LANES)
        of = slice(at, at + LANES)
        for z in range(nz):
            y32[t, pl.ds(z, ny, stride=nz), :] = y_ref[z, :, lanes].astype(F32)
        for j in range(1 + len(others)):
            for q in range(group):
                y = (low ^ j) * group + q
                z_term = others[j - 1][2 * q + h, :, of] if j else own_ref[2 * q + h, 0, :, of]
                y_term = y32[t, pl.ds(pl.multiple_of(y * nz, nz), nz), :]
                out_ref[y, :, lanes] = base_ref[y, :, lanes] + 0.5 * (y_term + z_term.astype(F32))


def body(scalars, velocity, first_x, second_x, first_y, second_y, first_z, second_z):
    _, ny, nz, nx = scalars.shape
    half = nx // 2
    blocks, lows = lax.axis_size("z"), lax.axis_size("m")
    cores = lax.axis_size("l") * lax.axis_size("c")
    peers = lax.axis_size("x") * cores
    high = lax.axis_index("h").reshape(1)
    low = lax.axis_index("m").reshape(1)
    s = scalars[0]
    whole = pl.BlockSpec((ny, nz, nx), lambda i: (0, 0, 0))

    def swap(array, axis, j):
        return lax.ppermute(array, axis, [(i, i ^ j) for i in range(lax.axis_size(axis))])

    def exchange(array, axes):
        return lax.all_to_all(array, axes, split_axis=0, concat_axis=0, tiled=True)

    def rows_split(matrix):
        return near(matrix.reshape(blocks, 2, ny, matrix.shape[1]))

    row_send = pl.pallas_call(
        pack_kernel,
        grid=(1,),
        in_specs=[whole, component(velocity.shape, 1)],
        out_specs=VMEM,
        out_shape=pltpu.VMEM((blocks, 2, ny, nx), BF16),
        scratch_shapes=[pltpu.VMEM((nx // LANES, ny * nz, LANES), F32)] * 2,
        name="pack",
    )(s, velocity)
    row_in = near(exchange(row_send, "z"))
    keep, *give = pl.pallas_call(
        pieces_kernel,
        grid=(1,),
        in_specs=[SMEM, whole, component(velocity.shape, 2)],
        out_specs=[VMEM] * lows,
        out_shape=[pltpu.VMEM((peers, 2, nz, half), BF16)] * lows,
        name="pieces",
    )(low, s, velocity)
    got = []
    for j, piece in enumerate(give, 1):
        got.append(near(swap(piece, "m", j)))
    col_send = pl.pallas_call(
        join_kernel,
        in_specs=[VMEM] * lows,
        out_specs=VMEM,
        out_shape=pltpu.VMEM((peers, lows, 2, nz, half), BF16),
        name="join",
    )(near(keep), *got)
    col_in = exchange(col_send, ("x", "l", "c"))
    own = pl.pallas_call(
        flux_kernel,
        in_specs=[VMEM],
        out_specs=VMEM,
        out_shape=pltpu.VMEM((2, blocks, ny, nx), BF16),
        name="flux",
    )(row_in)
    other = swap(own, "h", 1)
    base = pl.pallas_call(
        x_kernel,
        grid=(1,),
        in_specs=[whole, component(velocity.shape, 0), VMEM, VMEM],
        out_specs=VMEM,
        out_shape=pltpu.VMEM((ny, nz, nx), F32),
        name="xmath",
    )(s, velocity, near(first_x), near(second_x))
    rows = pl.pallas_call(
        rows_kernel,
        in_specs=[SMEM] + [VMEM] * 2,
        out_specs=VMEM,
        out_shape=pltpu.VMEM((2, blocks, ny, first_y.shape[1]), BF16),
        name="rows",
    )(high, rows_split(first_y), rows_split(second_y))
    z_term = pl.pallas_call(
        z_kernel,
        in_specs=[SMEM] + [VMEM] * 3,
        out_specs=VMEM,
        out_shape=pltpu.VMEM((peers, lows, nz, half), BF16),
        scratch_shapes=[
            pltpu.VMEM((2, peers // cores, lows, cores, nz, half), BF16),
            pltpu.VMEM((peers // cores, lows, cores, nz, half), BF16),
        ],
        name="zmath",
    )(low, near(col_in), near(first_z), near(second_z))
    z_back = exchange(z_term, ("x", "l", "c"))
    y_term = pl.pallas_call(
        y_kernel,
        in_specs=[SMEM] + [VMEM] * 4,
        out_specs=VMEM,
        out_shape=pltpu.VMEM((blocks, ny, nx), BF16),
        scratch_shapes=[pltpu.VMEM((2, blocks, 2, ny, nx), BF16)],
        name="ymath",
    )(high, row_in, near(own), near(other), near(rows))
    y_back = exchange(y_term, "z")
    returned = []
    for j in range(1, lows):
        returned.append(near(swap(z_back[:, j], "m", j)))
    out = pl.pallas_call(
        final_kernel,
        in_specs=[SMEM] + [VMEM] * (2 + lows),
        out_specs=VMEM,
        out_shape=jax.ShapeDtypeStruct((ny, nz, nx), F32),
        scratch_shapes=[pltpu.VMEM((nx // LANES, ny * nz, LANES), F32)],
        name="last",
    )(low, near(base), near(y_back), near(z_back), *returned)
    return out[None]


def solution(mesh):
    parts = Mesh(mesh.devices.reshape(8, 2, 4, 2, 2, 2), ("z", "h", "x", "m", "l", "c"))
    pencil = P(None, ("z", "h"), ("x", "m", "l", "c"), None)
    return jax.shard_map(
        body,
        mesh=parts,
        in_specs=(pencil, pencil, P(), P(), P(), P(), P(), P()),
        out_specs=pencil,
        check_vma=False,
    )
```

```python
import jax
import jax.numpy as jnp
from jax import lax
from jax.experimental import pallas as pl
from jax.experimental.pallas import tpu as pltpu
from jax.sharding import Mesh
from jax.sharding import PartitionSpec as P


LANES = 128
VMEM = pl.BlockSpec(memory_space=pltpu.VMEM)
SMEM = pl.BlockSpec(memory_space=pltpu.SMEM)
HBM = pl.BlockSpec(memory_space=pltpu.HBM)
BF16, F32 = jnp.bfloat16, jnp.float32


def component(shape, index):
    return pl.BlockSpec((None,) + shape[1:], lambda i: (index,) + (0,) * (len(shape) - 1))


def near(array):
    return pltpu.with_memory_space_constraint(array, pltpu.VMEM)


def far(array):
    return pltpu.with_memory_space_constraint(array, pltpu.HBM)


def dot(a, b, side):
    return lax.dot_general(a, b, (((1,), (side,)), ((), ())), preferred_element_type=F32)


def term_of(s, c, first, second, product):
    flux = (c * s.astype(F32)).astype(BF16)
    return -0.5 * (c * product(first, s) + product(first, flux)) + 0.5 * product(second, s)


def pack_kernel(low_ref, s_any, velocity_any, row_any, *rest):
    pieces, (s_ref, v_ref, w_ref, row_ref, s32, v32, sems) = rest[:-7], rest[-7:]
    ny, nz, nx = s_ref.shape
    half = nx // 2
    group = ny // len(pieces)
    low = low_ref[0]
    loads, stores = [], []
    for h in range(2):
        lanes = slice(h * half, (h + 1) * half)
        loads.append(pltpu.make_async_copy(s_any.at[:, :, lanes], s_ref.at[:, :, lanes], sems.at[h]))
        loads.append(pltpu.make_async_copy(velocity_any.at[1, :, :, lanes], v_ref.at[:, :, lanes], sems.at[2 + h]))
        stores.append(pltpu.make_async_copy(row_ref.at[:, :, :, lanes], row_any.at[:, :, :, lanes], sems.at[4 + h]))
    last = pltpu.make_async_copy(velocity_any.at[2], w_ref, sems.at[6])
    for copy in loads:
        copy.start()
    last.start()
    for h in range(2):
        loads[2 * h].wait()
        loads[2 * h + 1].wait()
        for t in range(h * half // LANES, (h + 1) * half // LANES):
            lanes = slice(t * LANES, (t + 1) * LANES)
            s32[t] = s_ref[:, :, lanes].reshape(ny * nz, LANES)
            v32[t] = v_ref[:, :, lanes].astype(F32).reshape(ny * nz, LANES)
            for z in range(nz):
                row_ref[z, 0, :, lanes] = s32[t, pl.ds(z, ny, stride=nz), :].astype(BF16)
                row_ref[z, 1, :, lanes] = v32[t, pl.ds(z, ny, stride=nz), :].astype(BF16)
        stores[h].start()
    last.wait()
    for j, piece in enumerate(pieces):
        for q in range(group):
            y = (low ^ j) * group + q
            for h in range(2):
                lanes = slice(h * half, (h + 1) * half)
                piece[2 * q + h, 0] = s_ref[y, :, lanes].astype(BF16)
                piece[2 * q + h, 1] = w_ref[y, :, lanes]
    for copy in stores:
        copy.wait()


def join_kernel(*refs):
    pieces, (out_any, sems) = refs[:-2], refs[-2:]
    copies = [pltpu.make_async_copy(piece, out_any.at[:, j], sems.at[j]) for j, piece in enumerate(pieces)]
    for copy in copies:
        copy.start()
    for copy in copies:
        copy.wait()


def flux_kernel(r_ref, out_ref):
    s = r_ref[:, 0]
    out_ref[0] = s
    out_ref[1] = (r_ref[:, 1].astype(F32) * s.astype(F32)).astype(BF16)


def x_kernel(s_ref, u_ref, first_ref, second_ref, out_ref):
    ny, nz, nx = s_ref.shape
    s = s_ref[...].reshape(ny * nz, nx)
    u = u_ref[...].astype(F32).reshape(ny * nz, nx)
    term = term_of(s.astype(BF16), u, first_ref[...], second_ref[...], lambda m, f: dot(f, m, 1))
    out_ref[...] = (s + 0.5 * term).reshape(ny, nz, nx)


def rows_kernel(high_ref, first_ref, second_ref, first_z_ref, second_z_ref, out_ref, z_ref):
    high = high_ref[0]
    out_ref[0] = first_ref[:, high]
    out_ref[1] = second_ref[:, high]
    z_ref[0] = first_z_ref[...]
    z_ref[1] = second_z_ref[...]


def y_kernel(high_ref, r_ref, own_ref, other_ref, rows_ref, out_ref, lines):
    _, blocks, depth, lanes = own_ref.shape
    high = high_ref[0]
    length = 2 * blocks * depth
    lines[:, :, high] = own_ref[...]
    lines[:, :, 1 - high] = other_ref[...]
    s = lines[0].reshape(length, lanes)
    flux = lines[1].reshape(length, lanes)
    first = rows_ref[0].reshape(blocks * depth, length)
    second = rows_ref[1].reshape(blocks * depth, length)
    c = r_ref[:, 1].reshape(blocks * depth, lanes).astype(F32)
    term = -0.5 * (c * dot(first, s, 0) + dot(first, flux, 0)) + 0.5 * dot(second, s, 0)
    out_ref[...] = term.astype(BF16).reshape(blocks, depth, lanes)


def z_kernel(low_ref, r_ref, operators_ref, out_ref, lines, terms):
    _, nx_blocks, lows, cores, depth, lanes = lines.shape
    low = low_ref[0]
    length = nx_blocks * lows * cores * depth
    for f in range(2):
        for x in range(nx_blocks):
            for j in range(lows):
                for c in range(cores):
                    lines[f, x, low ^ j, c] = r_ref[x * cores + c, j, f]
    s = lines[0].reshape(length, lanes)
    c = lines[1].reshape(length, lanes).astype(F32)
    term = term_of(s, c, operators_ref[0], operators_ref[1], lambda m, f: dot(m, f, 0))
    terms[...] = term.astype(BF16).reshape(terms.shape)
    for x in range(nx_blocks):
        for j in range(lows):
            for c in range(cores):
                out_ref[x * cores + c, j] = terms[x, low ^ j, c]


def final_kernel(low_ref, base_ref, y_ref, own_ref, *rest):
    others, (out_ref, y32) = rest[:-2], rest[-2:]
    ny, nz, nx = base_ref.shape
    half = nx // 2
    group = ny // (1 + len(others))
    low = low_ref[0]
    for t in range(nx // LANES):
        h, at = divmod(t * LANES, half)
        lanes = slice(t * LANES, (t + 1) * LANES)
        of = slice(at, at + LANES)
        for z in range(nz):
            y32[t, pl.ds(z, ny, stride=nz), :] = y_ref[z, :, lanes].astype(F32)
        for j in range(1 + len(others)):
            for q in range(group):
                y = (low ^ j) * group + q
                z_term = others[j - 1][2 * q + h, :, of] if j else own_ref[2 * q + h, 0, :, of]
                y_term = y32[t, pl.ds(pl.multiple_of(y * nz, nz), nz), :]
                out_ref[y, :, lanes] = base_ref[y, :, lanes] + 0.5 * (y_term + z_term.astype(F32))


def body(scalars, velocity, first_x, second_x, first_y, second_y, first_z, second_z):
    _, ny, nz, nx = scalars.shape
    half = nx // 2
    blocks, lows = lax.axis_size("z"), lax.axis_size("m")
    cores = lax.axis_size("l") * lax.axis_size("c")
    peers = lax.axis_size("x") * cores
    high = lax.axis_index("h").reshape(1)
    low = lax.axis_index("m").reshape(1)
    s = scalars[0]
    whole = pl.BlockSpec((ny, nz, nx), lambda i: (0, 0, 0))

    def swap(array, axis, j):
        return lax.ppermute(array, axis, [(i, i ^ j) for i in range(lax.axis_size(axis))])

    def exchange(array, axes):
        return lax.all_to_all(array, axes, split_axis=0, concat_axis=0, tiled=True)

    def rows_split(matrix):
        return near(matrix.reshape(blocks, 2, ny, matrix.shape[1]))

    row_send, keep, *give = pl.pallas_call(
        pack_kernel,
        in_specs=[SMEM, HBM, HBM],
        out_specs=[HBM] + [VMEM] * lows,
        out_shape=[pltpu.HBM((blocks, 2, ny, nx), BF16)] + [pltpu.VMEM((peers, 2, nz, half), BF16)] * lows,
        scratch_shapes=[
            pltpu.VMEM((ny, nz, nx), F32),
            pltpu.VMEM((ny, nz, nx), BF16),
            pltpu.VMEM((ny, nz, nx), BF16),
            pltpu.VMEM((blocks, 2, ny, nx), BF16),
            pltpu.VMEM((nx // LANES, ny * nz, LANES), F32),
            pltpu.VMEM((nx // LANES, ny * nz, LANES), F32),
            pltpu.SemaphoreType.DMA((7,)),
        ],
        name="pack",
    )(low, far(s), far(velocity))
    row_in = near(exchange(row_send, "z"))
    got = []
    for j, piece in enumerate(give, 1):
        got.append(near(swap(piece, "m", j)))
    col_send = pl.pallas_call(
        join_kernel,
        in_specs=[VMEM] * lows,
        out_specs=HBM,
        out_shape=pltpu.HBM((peers, lows, 2, nz, half), BF16),
        scratch_shapes=[pltpu.SemaphoreType.DMA((lows,))],
        name="join",
    )(near(keep), *got)
    own = pl.pallas_call(
        flux_kernel,
        in_specs=[VMEM],
        out_specs=VMEM,
        out_shape=pltpu.VMEM((2, blocks, ny, nx), BF16),
        name="flux",
    )(row_in)
    col_send, own = lax.optimization_barrier((col_send, own))
    col_in = exchange(col_send, ("x", "l", "c"))
    other = swap(own, "h", 1)
    base = pl.pallas_call(
        x_kernel,
        grid=(1,),
        in_specs=[whole, component(velocity.shape, 0), VMEM, VMEM],
        out_specs=VMEM,
        out_shape=pltpu.VMEM((ny, nz, nx), F32),
        name="xmath",
    )(s, velocity, near(first_x), near(second_x))
    rows, z_operators = pl.pallas_call(
        rows_kernel,
        in_specs=[SMEM] + [VMEM] * 4,
        out_specs=[VMEM] * 2,
        out_shape=[
            pltpu.VMEM((2, blocks, ny, first_y.shape[1]), BF16),
            pltpu.VMEM((2,) + first_z.shape, BF16),
        ],
        name="rows",
    )(high, rows_split(first_y), rows_split(second_y), near(first_z), near(second_z))
    z_term = pl.pallas_call(
        z_kernel,
        in_specs=[SMEM] + [VMEM] * 2,
        out_specs=VMEM,
        out_shape=pltpu.VMEM((peers, lows, nz, half), BF16),
        scratch_shapes=[
            pltpu.VMEM((2, peers // cores, lows, cores, nz, half), BF16),
            pltpu.VMEM((peers // cores, lows, cores, nz, half), BF16),
        ],
        name="zmath",
    )(low, near(col_in), near(z_operators))
    z_back = exchange(z_term, ("x", "l", "c"))
    y_term = pl.pallas_call(
        y_kernel,
        in_specs=[SMEM] + [VMEM] * 4,
        out_specs=VMEM,
        out_shape=pltpu.VMEM((blocks, ny, nx), BF16),
        scratch_shapes=[pltpu.VMEM((2, blocks, 2, ny, nx), BF16)],
        name="ymath",
    )(high, row_in, near(own), near(other), near(rows))
    y_back = exchange(y_term, "z")
    returned = []
    for j in range(1, lows):
        returned.append(near(swap(z_back[:, j], "m", j)))
    out = pl.pallas_call(
        final_kernel,
        in_specs=[SMEM] + [VMEM] * (2 + lows),
        out_specs=VMEM,
        out_shape=jax.ShapeDtypeStruct((ny, nz, nx), F32),
        scratch_shapes=[pltpu.VMEM((nx // LANES, ny * nz, LANES), F32)],
        name="last",
    )(low, near(base), near(y_back), near(z_back), *returned)
    return out[None]


def solution(mesh):
    parts = Mesh(mesh.devices.reshape(8, 2, 4, 2, 2, 2), ("z", "h", "x", "m", "l", "c"))
    pencil = P(None, ("z", "h"), ("x", "m", "l", "c"), None)
    return jax.shard_map(
        body,
        mesh=parts,
        in_specs=(pencil, pencil, P(), P(), P(), P(), P(), P()),
        out_specs=pencil,
        check_vma=False,
    )
```

```python
import jax
import jax.numpy as jnp
from jax import lax
from jax.experimental import pallas as pl
from jax.experimental.pallas import tpu as pltpu
from jax.sharding import Mesh
from jax.sharding import PartitionSpec as P


LANES = 128
VMEM = pl.BlockSpec(memory_space=pltpu.VMEM)
SMEM = pl.BlockSpec(memory_space=pltpu.SMEM)
HBM = pl.BlockSpec(memory_space=pltpu.HBM)
BF16, F32 = jnp.bfloat16, jnp.float32


def component(shape, index):
    return pl.BlockSpec((None,) + shape[1:], lambda i: (index,) + (0,) * (len(shape) - 1))


def near(array):
    return pltpu.with_memory_space_constraint(array, pltpu.VMEM)


def far(array):
    return pltpu.with_memory_space_constraint(array, pltpu.HBM)


def dot(a, b, side):
    return lax.dot_general(a, b, (((1,), (side,)), ((), ())), preferred_element_type=F32)


def term_of(s, c, first, second, product):
    flux = (c * s.astype(F32)).astype(BF16)
    return -0.5 * (c * product(first, s) + product(first, flux)) + 0.5 * product(second, s)


def pack_kernel(low_ref, s_any, velocity_any, row_any, *rest):
    pieces, (s_ref, v_ref, w_ref, row_ref, s32, v32, sems) = rest[:-7], rest[-7:]
    ny, nz, nx = s_ref.shape
    half = nx // 2
    group = ny // len(pieces)
    low = low_ref[0]
    loads, stores = [], []
    for h in range(2):
        lanes = slice(h * half, (h + 1) * half)
        loads.append(pltpu.make_async_copy(s_any.at[:, :, lanes], s_ref.at[:, :, lanes], sems.at[h]))
        loads.append(pltpu.make_async_copy(velocity_any.at[1, :, :, lanes], v_ref.at[:, :, lanes], sems.at[2 + h]))
        stores.append(pltpu.make_async_copy(row_ref.at[:, :, :, lanes], row_any.at[:, :, :, lanes], sems.at[4 + h]))
    last = pltpu.make_async_copy(velocity_any.at[2], w_ref, sems.at[6])
    for copy in loads:
        copy.start()
    last.start()
    for h in range(2):
        loads[2 * h].wait()
        loads[2 * h + 1].wait()
        for t in range(h * half // LANES, (h + 1) * half // LANES):
            lanes = slice(t * LANES, (t + 1) * LANES)
            s32[t] = s_ref[:, :, lanes].reshape(ny * nz, LANES)
            v32[t] = v_ref[:, :, lanes].astype(F32).reshape(ny * nz, LANES)
            for z in range(nz):
                row_ref[z, 0, :, lanes] = s32[t, pl.ds(z, ny, stride=nz), :].astype(BF16)
                row_ref[z, 1, :, lanes] = v32[t, pl.ds(z, ny, stride=nz), :].astype(BF16)
        stores[h].start()
    last.wait()
    for j, piece in enumerate(pieces):
        for q in range(group):
            y = (low ^ j) * group + q
            for h in range(2):
                lanes = slice(h * half, (h + 1) * half)
                piece[2 * q + h, 0] = s_ref[y, :, lanes].astype(BF16)
                piece[2 * q + h, 1] = w_ref[y, :, lanes]
    for copy in stores:
        copy.wait()


def join_kernel(*refs):
    pieces, (out_any, sems) = refs[:-2], refs[-2:]
    copies = [pltpu.make_async_copy(piece, out_any.at[:, j], sems.at[j]) for j, piece in enumerate(pieces)]
    for copy in copies:
        copy.start()
    for copy in copies:
        copy.wait()


def flux_kernel(r_ref, out_ref):
    s = r_ref[:, 0]
    out_ref[0] = s
    out_ref[1] = (r_ref[:, 1].astype(F32) * s.astype(F32)).astype(BF16)


def x_kernel(s_ref, u_ref, first_ref, second_ref, out_ref):
    ny, nz, nx = s_ref.shape
    s = s_ref[...].reshape(ny * nz, nx)
    u = u_ref[...].astype(F32).reshape(ny * nz, nx)
    term = term_of(s.astype(BF16), u, first_ref[...], second_ref[...], lambda m, f: dot(f, m, 1))
    out_ref[...] = (s + 0.5 * term).reshape(ny, nz, nx)


def rows_kernel(high_ref, first_ref, second_ref, first_z_ref, second_z_ref, out_ref, z_ref):
    high = high_ref[0]
    out_ref[0] = first_ref[:, high]
    out_ref[1] = second_ref[:, high]
    z_ref[0] = first_z_ref[...]
    z_ref[1] = second_z_ref[...]


def y_kernel(high_ref, r_ref, own_ref, other_ref, rows_ref, out_any, lines, out_ref, sems):
    _, blocks, depth, width = own_ref.shape
    high = high_ref[0]
    length = 2 * blocks * depth
    first = rows_ref[0].reshape(blocks * depth, length)
    second = rows_ref[1].reshape(blocks * depth, length)
    half = width // 2
    copies = []
    for part in range(2):
        lanes = slice(part * half, (part + 1) * half)
        lines[:, :, high] = own_ref[:, :, :, lanes]
        lines[:, :, 1 - high] = other_ref[:, :, :, lanes]
        s = lines[0].reshape(length, half)
        flux = lines[1].reshape(length, half)
        c = r_ref[:, 1, :, lanes].reshape(blocks * depth, half).astype(F32)
        term = -0.5 * (c * dot(first, s, 0) + dot(first, flux, 0)) + 0.5 * dot(second, s, 0)
        out_ref[:, :, lanes] = term.astype(BF16).reshape(blocks, depth, half)
        copies.append(pltpu.make_async_copy(out_ref.at[:, :, lanes], out_any.at[:, :, lanes], sems.at[part]))
        copies[part].start()
    for copy in copies:
        copy.wait()


def z_kernel(low_ref, r_ref, operators_ref, out_ref, lines, terms):
    _, nx_blocks, lows, cores, depth, lanes = lines.shape
    low = low_ref[0]
    length = nx_blocks * lows * cores * depth
    for f in range(2):
        for x in range(nx_blocks):
            for j in range(lows):
                for c in range(cores):
                    lines[f, x, low ^ j, c] = r_ref[x * cores + c, j, f]
    s = lines[0].reshape(length, lanes)
    c = lines[1].reshape(length, lanes).astype(F32)
    term = term_of(s, c, operators_ref[0], operators_ref[1], lambda m, f: dot(m, f, 0))
    terms[...] = term.astype(BF16).reshape(terms.shape)
    for x in range(nx_blocks):
        for j in range(lows):
            for c in range(cores):
                out_ref[x * cores + c, j] = terms[x, low ^ j, c]


def final_kernel(low_ref, base_ref, y_ref, own_ref, *rest):
    others, (out_ref, y32) = rest[:-2], rest[-2:]
    ny, nz, nx = base_ref.shape
    half = nx // 2
    group = ny // (1 + len(others))
    low = low_ref[0]
    for t in range(nx // LANES):
        h, at = divmod(t * LANES, half)
        lanes = slice(t * LANES, (t + 1) * LANES)
        of = slice(at, at + LANES)
        for z in range(nz):
            y32[t, pl.ds(z, ny, stride=nz), :] = y_ref[z, :, lanes].astype(F32)
        for j in range(1 + len(others)):
            for q in range(group):
                y = (low ^ j) * group + q
                z_term = others[j - 1][2 * q + h, :, of] if j else own_ref[2 * q + h, 0, :, of]
                y_term = y32[t, pl.ds(pl.multiple_of(y * nz, nz), nz), :]
                out_ref[y, :, lanes] = base_ref[y, :, lanes] + 0.5 * (y_term + z_term.astype(F32))


def body(scalars, velocity, first_x, second_x, first_y, second_y, first_z, second_z):
    _, ny, nz, nx = scalars.shape
    half = nx // 2
    blocks, lows = lax.axis_size("z"), lax.axis_size("m")
    cores = lax.axis_size("l") * lax.axis_size("c")
    peers = lax.axis_size("x") * cores
    high = lax.axis_index("h").reshape(1)
    low = lax.axis_index("m").reshape(1)
    s = scalars[0]
    whole = pl.BlockSpec((ny, nz, nx), lambda i: (0, 0, 0))

    def swap(array, axis, j):
        return lax.ppermute(array, axis, [(i, i ^ j) for i in range(lax.axis_size(axis))])

    def exchange(array, axes):
        return lax.all_to_all(array, axes, split_axis=0, concat_axis=0, tiled=True)

    def rows_split(matrix):
        return near(matrix.reshape(blocks, 2, ny, matrix.shape[1]))

    row_send, keep, *give = pl.pallas_call(
        pack_kernel,
        in_specs=[SMEM, HBM, HBM],
        out_specs=[HBM] + [VMEM] * lows,
        out_shape=[pltpu.HBM((blocks, 2, ny, nx), BF16)] + [pltpu.VMEM((peers, 2, nz, half), BF16)] * lows,
        scratch_shapes=[
            pltpu.VMEM((ny, nz, nx), F32),
            pltpu.VMEM((ny, nz, nx), BF16),
            pltpu.VMEM((ny, nz, nx), BF16),
            pltpu.VMEM((blocks, 2, ny, nx), BF16),
            pltpu.VMEM((nx // LANES, ny * nz, LANES), F32),
            pltpu.VMEM((nx // LANES, ny * nz, LANES), F32),
            pltpu.SemaphoreType.DMA((7,)),
        ],
        name="pack",
    )(low, far(s), far(velocity))
    row_in = near(exchange(row_send, "z"))
    got = []
    for j, piece in enumerate(give, 1):
        got.append(near(swap(piece, "m", j)))
    col_send = pl.pallas_call(
        join_kernel,
        in_specs=[VMEM] * lows,
        out_specs=HBM,
        out_shape=pltpu.HBM((peers, lows, 2, nz, half), BF16),
        scratch_shapes=[pltpu.SemaphoreType.DMA((lows,))],
        name="join",
    )(near(keep), *got)
    own = pl.pallas_call(
        flux_kernel,
        in_specs=[VMEM],
        out_specs=VMEM,
        out_shape=pltpu.VMEM((2, blocks, ny, nx), BF16),
        name="flux",
    )(row_in)
    col_send, own = lax.optimization_barrier((col_send, own))
    col_in = exchange(col_send, ("x", "l", "c"))
    other = swap(own, "h", 1)
    base = pl.pallas_call(
        x_kernel,
        grid=(1,),
        in_specs=[whole, component(velocity.shape, 0), VMEM, VMEM],
        out_specs=VMEM,
        out_shape=pltpu.VMEM((ny, nz, nx), F32),
        name="xmath",
    )(s, velocity, near(first_x), near(second_x))
    rows, z_operators = pl.pallas_call(
        rows_kernel,
        in_specs=[SMEM] + [VMEM] * 4,
        out_specs=[VMEM] * 2,
        out_shape=[
            pltpu.VMEM((2, blocks, ny, first_y.shape[1]), BF16),
            pltpu.VMEM((2,) + first_z.shape, BF16),
        ],
        name="rows",
    )(high, rows_split(first_y), rows_split(second_y), near(first_z), near(second_z))
    z_term = pl.pallas_call(
        z_kernel,
        in_specs=[SMEM] + [VMEM] * 2,
        out_specs=VMEM,
        out_shape=pltpu.VMEM((peers, lows, nz, half), BF16),
        scratch_shapes=[
            pltpu.VMEM((2, peers // cores, lows, cores, nz, half), BF16),
            pltpu.VMEM((peers // cores, lows, cores, nz, half), BF16),
        ],
        name="zmath",
    )(low, near(col_in), near(z_operators))
    z_back = exchange(z_term, ("x", "l", "c"))
    y_term = pl.pallas_call(
        y_kernel,
        in_specs=[SMEM] + [VMEM] * 4,
        out_specs=HBM,
        out_shape=pltpu.HBM((blocks, ny, nx), BF16),
        scratch_shapes=[
            pltpu.VMEM((2, blocks, 2, ny, half), BF16),
            pltpu.VMEM((blocks, ny, nx), BF16),
            pltpu.SemaphoreType.DMA((2,)),
        ],
        name="ymath",
    )(high, row_in, near(own), near(other), near(rows))
    y_back = exchange(y_term, "z")
    returned = []
    for j in range(1, lows):
        returned.append(near(swap(z_back[:, j], "m", j)))
    out = pl.pallas_call(
        final_kernel,
        in_specs=[SMEM] + [VMEM] * (2 + lows),
        out_specs=VMEM,
        out_shape=jax.ShapeDtypeStruct((ny, nz, nx), F32),
        scratch_shapes=[pltpu.VMEM((nx // LANES, ny * nz, LANES), F32)],
        name="last",
    )(low, near(base), near(y_back), near(z_back), *returned)
    return out[None]


def solution(mesh):
    parts = Mesh(mesh.devices.reshape(8, 2, 4, 2, 2, 2), ("z", "h", "x", "m", "l", "c"))
    pencil = P(None, ("z", "h"), ("x", "m", "l", "c"), None)
    return jax.shard_map(
        body,
        mesh=parts,
        in_specs=(pencil, pencil, P(), P(), P(), P(), P(), P()),
        out_specs=pencil,
        check_vma=False,
    )
```
